32 devices in a mesh: dirs: 2 (over y), taps: 4 (over z), tm: 2 (over x), floors: 2 (over core).
Axes of the slice: x: 2, y: 2, z: 4, core: 2. Of those that a mesh axis runs over, the one named last changes fastest.
Arguments:
- pressures: bfloat16 [4096, 16384], P(('dirs', 'tm'), ('taps', 'floors')), parts along dimension 0, may hold values from -6 to 6
- tap_area: bfloat16 [16384], P(('taps', 'floors')), may hold values from 0.29882812 to 3
- tap_panel: int32 [16384], P(('taps', 'floors')), may hold values from 0 to 255
- tap_floor: int32 [16384], P(('taps', 'floors')), may hold values from 0 to 15
- panel_shape: bfloat16 [256, 512], replicated, may hold values from -0.046875 to 0.046875
- floor_shape: bfloat16 [16, 512], replicated, may hold values from -0.25 to 0.25
- mode_order: int32 [512], replicated, may hold values from 0 to 511, each once
- mode_decay: float32 [512], replicated, may hold values from 4.8828125e-05 to 0.08
- mode_freq: float32 [512], replicated, may hold values from 0.02 to 1.2
Outputs:
- modal_response: float32 [512, 4096], P(('taps', 'floors'), ('dirs', 'tm')), parts along dimension 1
- floor_motion: float32 [16, 4096], P(('taps', 'floors'), ('dirs', 'tm')), parts along dimension 1
- floor_load: float32 [16, 4096], P(('taps', 'floors'), ('dirs', 'tm')), parts along dimension 1
The draws below stay inside these ranges and needn't reach their ends.
There are 2 independent parts, one for each index of `dirs`. The reference program is written for one: setup_inputs(seed, part) draws one part's arguments, and reference() takes and returns one part's arrays. A program takes and returns all parts, laid end to end along the dimension named above; an argument that names none is the same for every part. Nothing has to cross between parts.
All inputs are finite; a program needn't handle non-finite values.
Results may differ from the reference program's by a relative error of at most 0.0029.
Values sent between devices are 32-bit elements; how exact they have to be, the bound alone decides.
A program may use at most 64 MiB of HBM per device.

```python
import math
import jax
import jax.numpy as jnp
from jax import lax

M = 512
PANELS = 256
TAP_DEV = 2048
TIME = 2048
TAPS = 16384
FLOORS = 16


def draw_mode_decay(key, part):
    key_pick = jax.random.fold_in(key, 11)
    key_slow = jax.random.fold_in(key, 12)
    key_fast = jax.random.fold_in(key, 13)
    slow_share = 0.5
    slow_pick = jax.random.uniform(key_pick, (M,), jnp.float32) < slow_share
    slow_rates = 0.1 / TIME * jnp.exp(jax.random.uniform(key_slow, (M,), jnp.float32, 0.0, math.log(10.0)))
    fast_rates = jnp.exp(jax.random.uniform(key_fast, (M,), jnp.float32, math.log(0.02), math.log(0.08)))
    return jnp.where(slow_pick, slow_rates, fast_rates).astype(jnp.float32)


def touch_ends(values, own_key, least, largest):
    extent = values.shape
    index_at = [jax.random.randint(jax.random.fold_in(own_key, axis), (), 0, extent[axis]) for axis in range(len(extent))]
    values = values.at[tuple(index_at)].set(least)
    longest = extent.index(max(extent))
    index_at[longest] = (index_at[longest] + 1) % extent[longest]
    return values.at[tuple(index_at)].set(largest)


def block_levels(stream_key, shape, cuts, least, largest):
    level, own = 1.0, jax.random.fold_in(stream_key, 6)
    for position, blocks in cuts:
        heights = jnp.exp(jax.random.uniform(jax.random.fold_in(own, position), (blocks,), jnp.float32, least / len(cuts), largest / len(cuts)))
        level = level * jnp.repeat(heights, shape[position] // blocks).reshape([-1 if axis == position else 1 for axis in range(len(shape))])
    return level


def noise(own_key, extent, spread, limit, shards=(), held_as=jnp.bfloat16):
    result = spread * jax.random.normal(own_key, extent, jnp.float32)
    if shards:
        result = result * block_levels(own_key, extent, shards, -0.22, 0.18)
    return jnp.clip(result, -limit, limit).astype(held_as)


def setup_inputs(seed: int = 0, part: int = 0) -> dict:
    streams_of = jax.random.split(jax.random.key(seed), 10)
    own_keys = jax.random.split(jax.random.fold_in(streams_of[9], part), 10)
    pressures = noise(own_keys[0], (TIME, TAPS), 1.0, 6.0, ((0, 2), (1, 8)))
    tap_area = jnp.clip(jnp.exp(math.log(3.0) - 2.306499 * jax.random.uniform(streams_of[1], (TAPS,), jnp.float32) ** block_levels(streams_of[1], (TAPS,), ((0, 8),), -0.2, 0.2)), 0.29882812, 3.0).astype(jnp.bfloat16)
    tap_panel = touch_ends(jax.random.randint(streams_of[2], (TAPS,), 0, PANELS), jax.random.fold_in(streams_of[2], 1), 0, PANELS - 1).astype(jnp.int32)
    tap_floor = touch_ends(jax.random.randint(streams_of[3], (TAPS,), 0, FLOORS), jax.random.fold_in(streams_of[3], 1), 0, FLOORS - 1).astype(jnp.int32)
    panel_shape = noise(streams_of[4], (PANELS, M), TAPS ** -0.5, 0.046875)
    floor_shape = noise(streams_of[5], (FLOORS, M), M ** -0.5, 0.25)
    mode_order = jax.random.permutation(streams_of[6], M).astype(jnp.int32)
    mode_decay = draw_mode_decay(jax.random.fold_in(streams_of[9], 71), part)
    mode_freq = jnp.clip(jnp.exp(jax.random.uniform(streams_of[8], (M,), jnp.float32, math.log(0.02), math.log(1.2))), 0.02, 1.2)
    return {"pressures": pressures, "tap_area": tap_area, "tap_panel": tap_panel, "tap_floor": tap_floor, "panel_shape": panel_shape, "floor_shape": floor_shape, "mode_order": mode_order, "mode_decay": mode_decay, "mode_freq": mode_freq}


def reference(pressures, tap_area, tap_panel, tap_floor, panel_shape, floor_shape, mode_order, mode_decay, mode_freq):
    ordered = jnp.take(panel_shape, mode_order, axis=1)
    floor_ids = jnp.arange(FLOORS, dtype=jnp.int32)
    block_count = TAPS // TAP_DEV

    def accumulate(carried, block_idx):
        start = (block_idx * TAP_DEV).astype(jnp.int32)
        window = lax.dynamic_slice_in_dim(pressures, start, TAP_DEV, 1)
        area_block = lax.dynamic_slice_in_dim(tap_area, start, TAP_DEV, 0)
        panel_block = lax.dynamic_slice_in_dim(tap_panel, start, TAP_DEV, 0)
        floor_block = lax.dynamic_slice_in_dim(tap_floor, start, TAP_DEV, 0)
        tributary = (jnp.take(ordered, panel_block, axis=0).astype(jnp.float32) * area_block.astype(jnp.float32)[:, None]).astype(jnp.bfloat16)
        forces = carried[0] + lax.dot_general(tributary, window, (((0,), (1,)), ((), ())), preferred_element_type=jnp.float32)
        weights = jnp.where(floor_block[None, :] == floor_ids[:, None], area_block[None, :], jnp.zeros((), jnp.bfloat16))
        loads = carried[1] + lax.dot_general(weights, window, (((1,), (1,)), ((), ())), preferred_element_type=jnp.float32)
        return ((forces, loads), None)
    start_sums = (jnp.zeros((M, TIME), jnp.float32), jnp.zeros((FLOORS, TIME), jnp.float32))
    (forces, loads), _ = lax.scan(accumulate, start_sums, jnp.arange(block_count, dtype=jnp.int32))
    decays = jnp.take(mode_decay, mode_order)
    angles = jnp.take(mode_freq, mode_order)
    input_gain = jnp.sqrt(-jnp.expm1(-2.0 * decays))
    turn_re = jnp.exp(-decays) * jnp.cos(angles)
    turn_im = jnp.exp(-decays) * jnp.sin(angles)

    def advance(carried, force_now):
        real_part, imag_part = carried
        next_real = turn_re * real_part - turn_im * imag_part + input_gain * force_now
        next_imag = turn_im * real_part + turn_re * imag_part
        return ((next_real, next_imag), next_real)
    zeros_state = jnp.zeros((M,), jnp.float32)
    _, history = lax.scan(advance, (zeros_state, zeros_state), forces.T)
    motion = history.T
    local_shape = jnp.take(floor_shape, mode_order, axis=1).astype(jnp.float32)
    floor_motion = jnp.dot(local_shape, motion, precision=lax.Precision.HIGHEST, preferred_element_type=jnp.float32)
    floor_load = loads * (FLOORS / TAPS) ** 0.5
    return (motion, floor_motion, floor_load)
```

```python
import functools

import jax
import jax.numpy as jnp
from jax import lax
from jax.experimental import pallas as pl
from jax.experimental.pallas import tpu as pltpu
from jax.sharding import PartitionSpec as P

MESH = pl.DeviceIdType.MESH
LANES = 128
LAG = 2
NT = (((1,), (1,)), ((), ()))


def dot_nt(a, b):
    return lax.dot_general(a, b, NT, preferred_element_type=jnp.float32)


def dot_split(a, b):
    hi = b.astype(jnp.bfloat16)
    lo = (b - hi.astype(jnp.float32)).astype(jnp.bfloat16)
    return jnp.dot(a, hi, preferred_element_type=jnp.float32) + jnp.dot(
        a, lo, preferred_element_type=jnp.float32
    )


def kernel(
    cfg,
    p_hbm, area_ref, panel_ref, floor_ref, shape_ref, fshape_ref, order_ref, decay_ref, freq_ref,
    y_ref, fm_ref, fl_ref,
    pv, w_ref, mine, send_p, recv_p, rin, lin, rout, lout, xs, fb, tabs, loc, st_send, st_recv,
    fs, fr,
    p_sem, pp_s, pp_r, r_s, r_r, l_s, l_r, x_s, x_r, t_s, t_r, f_s, f_r,
):
    nz, nc, ntm, splits = cfg
    owners = nz * nc
    z = lax.axis_index("taps")
    c = lax.axis_index("floors")
    x = lax.axis_index("tm")
    me = z * nc + c
    other = nc - 1 - c
    time_dev, taps = pv.shape
    panels, modes = shape_ref.shape
    floors = fshape_ref.shape[0]
    rows = panels + floors
    th = time_dev // nc
    tblocks = th // LANES
    crows = rows // splits
    nch = tblocks * splits
    md = modes // owners
    fd = floors // owners
    f32 = jnp.float32
    bf16 = jnp.bfloat16

    barrier = pltpu.get_barrier_semaphore()

    def greet(k, carry):
        j = lax.rem(me + k, owners)
        pl.semaphore_signal(
            barrier, inc=1, device_id={"taps": j // nc, "floors": lax.rem(j, nc)}, device_id_type=MESH
        )
        return carry

    lax.fori_loop(1, owners, greet, 0)
    for k in range(1, ntm):
        pl.semaphore_signal(
            barrier, inc=1, device_id={"tm": lax.rem(x + k, ntm)}, device_id_type=MESH
        )

    step_t = min(256, th)
    per_half = th // step_t
    loads = []
    for h in range(2):
        half = other if h == 0 else c
        for b in range(per_half):
            off = pl.multiple_of(half * th + b * step_t, step_t)
            cp = pltpu.make_async_copy(
                p_hbm.at[pl.ds(off, step_t)], pv.at[pl.ds(off, step_t)], p_sem.at[h * per_half + b]
            )
            cp.start()
            loads.append((cp, off))

    area = area_ref[...].astype(f32)
    ids = lax.broadcasted_iota(jnp.int32, (panels, taps), 0)
    w_ref[0:panels, :] = jnp.where(panel_ref[...] == ids, area, 0.0).astype(bf16)
    fids = lax.broadcasted_iota(jnp.int32, (floors, taps), 0)
    w_ref[panels:rows, :] = jnp.where(floor_ref[...] == fids, area, 0.0).astype(bf16)

    def sums(b, h, dst):
        cp, off = loads[h * per_half + b]
        cp.wait()
        q = dot_nt(w_ref[...], pv[pl.ds(off, step_t), :])
        for i in range(step_t // LANES):
            for s in range(splits):
                dst[(b * step_t // LANES + i) * splits + s] = q[
                    s * crows : (s + 1) * crows, i * LANES : (i + 1) * LANES
                ]

    def pair_copy(k):
        return pltpu.make_async_remote_copy(
            src_ref=send_p.at[k], dst_ref=recv_p.at[k], send_sem=pp_s.at[k], recv_sem=pp_r.at[k],
            device_id={"floors": other}, device_id_type=MESH,
        )

    per_step = step_t // LANES * splits
    for b in range(per_half):
        sums(b, 0, send_p)
        if b == 0:
            pl.semaphore_wait(barrier, owners - 1 + ntm - 1)
        for k in range(b * per_step, (b + 1) * per_step):
            pair_copy(k).start()
    for b in range(per_half):
        sums(b, 1, mine)

    @pl.when(z == 0)
    def _():
        rin[...] = jnp.zeros_like(rin)

    @pl.when(z == nz - 1)
    def _():
        lin[...] = jnp.zeros_like(lin)

    for k in range(nch):
        pair_copy(k).wait_recv()
        mine[k] = mine[k] + recv_p[k]

    def line_copy(k, right):
        src, dst, ss, rs = (rout, rin, r_s, r_r) if right else (lout, lin, l_s, l_r)
        to = jnp.minimum(z + 1, nz - 1) if right else jnp.maximum(z - 1, 0)
        return pltpu.make_async_remote_copy(
            src_ref=src.at[k], dst_ref=dst.at[k], send_sem=ss.at[k], recv_sem=rs.at[k],
            device_id={"taps": to}, device_id_type=MESH,
        )

    def line_step(s, carry):
        for right in (True, False):
            hop = z if right else nz - 1 - z
            k = s - LAG * hop
            came, out = (rin, rout) if right else (lin, lout)

            @pl.when(jnp.logical_and(k >= 0, k < nch))
            def _():
                @pl.when(hop > 0)
                def _():
                    line_copy(k, right).wait_recv()

                @pl.when(hop < nz - 1)
                def _():
                    out[k] = mine[k] + came[k]
                    line_copy(k, right).start()

        return carry

    lax.fori_loop(0, nch + LAG * (nz - 1), line_step, 0)

    mode_ids = lax.broadcasted_iota(jnp.int32, (md, modes), 1)

    def pick(owner):
        mine_order = order_ref[pl.ds(pl.multiple_of(owner * md, md), md), :]
        return mine_order == mode_ids

    def shapes(hot):
        return dot_nt(hot.astype(f32).astype(bf16), shape_ref[...]).astype(bf16)

    hot_me = pick(me)
    hot_other = pick(z * nc + other)
    g_both = jnp.concatenate([shapes(hot_other), shapes(hot_me)], axis=0)
    d = jnp.sum(jnp.where(hot_me, decay_ref[...], 0.0), axis=1, keepdims=True)
    w = jnp.sum(jnp.where(hot_me, freq_ref[...], 0.0), axis=1, keepdims=True)
    ls = dot_nt(fshape_ref[...], hot_me.astype(f32).astype(bf16)).astype(bf16)
    e2 = 2.0 * d
    series = 1.0 / 40320.0
    poly = jnp.full_like(e2, series)
    for coef in (1.0 / 5040, 1.0 / 720, 1.0 / 120, 1.0 / 24, 1.0 / 6, 0.5, 1.0):
        poly = coef - e2 * poly
    gain = jnp.sqrt(e2 * poly)
    ahead = (lax.broadcasted_iota(jnp.int32, (md, LANES), 1) + 1).astype(f32)
    mag = jnp.exp(-d * ahead)
    t_re = mag * jnp.cos(w * ahead)
    t_im = mag * jnp.sin(w * ahead)
    tabs[0] = t_re
    tabs[1] = t_im
    lane = lax.broadcasted_iota(jnp.int32, (md, LANES), 1)

    floor_row = lax.broadcasted_iota(jnp.int32, (floors, LANES), 0)

    def pick_loads(q, owner, lo):
        for r in range(fd):
            lo.append(jnp.sum(jnp.where(floor_row == owner * fd + r, q, 0.0), axis=0, keepdims=True))

    for tb in range(tblocks):
        parts = []
        for s in range(splits):
            k = tb * splits + s
            parts.append(mine[k] + rin[k] + lin[k])
        q = jnp.concatenate(parts, axis=0)
        both = dot_split(g_both, q[:panels])
        cols = slice(tb * LANES, (tb + 1) * LANES)
        xs[0:md, cols] = both[:md]
        fb[c, 0:md, cols] = both[md:]
        theirs, ours = [], []
        pick_loads(q[panels:], z * nc + other, theirs)
        pick_loads(q[panels:], me, ours)
        for r in range(fd):
            xs[md + r : md + r + 1, cols] = theirs[r]
            fb[c, md + r : md + r + 1, cols] = ours[r]
    pad = xs.shape[0] - md - fd
    if pad:
        xs[md + fd :, :] = jnp.zeros((pad, th), f32)
        fb[c, md + fd :, :] = jnp.zeros((pad, th), f32)
    ex = pltpu.make_async_remote_copy(
        src_ref=xs, dst_ref=fb.at[c], send_sem=x_s, recv_sem=x_r,
        device_id={"floors": other}, device_id_type=MESH,
    )
    ex.start()
    ex.wait_recv()

    end_re, end_im = [], []
    coefs = []
    step = 1
    while step < LANES:
        keep = lane >= step
        coefs.append(
            (
                step,
                jnp.where(keep, t_re[:, step - 1 : step], 0.0),
                jnp.where(keep, t_im[:, step - 1 : step], 0.0),
            )
        )
        step *= 2
    for i, (_, a, b) in enumerate(coefs):
        tabs[2 + 2 * i] = a
        tabs[3 + 2 * i] = b
    nb = time_dev // LANES
    for blk in range(nb):
        h, tb = blk // tblocks, blk % tblocks
        re = gain * fb[h, 0:md, tb * LANES : (tb + 1) * LANES]
        im = None
        for i, (step, _, _) in enumerate(coefs):
            a, b = tabs[2 + 2 * i], tabs[3 + 2 * i]
            rr = pltpu.roll(re, step, 1)
            if im is None:
                re, im = re + a * rr, b * rr
            else:
                ri = pltpu.roll(im, step, 1)
                re, im = re + a * rr - b * ri, im + a * ri + b * rr
        loc[blk] = re
        end_re.append(re[:, LANES - 1 :])
        end_im.append(im[:, LANES - 1 :])

    zb_re, zb_im = t_re[:, LANES - 1 :], t_im[:, LANES - 1 :]
    s_re, s_im = end_re[0], end_im[0]
    for blk in range(1, nb):
        s_re, s_im = (
            zb_re * s_re - zb_im * s_im + end_re[blk],
            zb_im * s_re + zb_re * s_im + end_im[blk],
        )

    def state_copy(to, src):
        return pltpu.make_async_remote_copy(
            src_ref=st_send, dst_ref=st_recv.at[src], send_sem=t_s.at[to], recv_sem=t_r.at[src],
            device_id={"tm": to}, device_id_type=MESH,
        )

    st_send[...] = jnp.where(lane == 0, s_re, s_im)
    in_re = jnp.zeros((md, 1), f32)
    in_im = jnp.zeros((md, 1), f32)
    if ntm > 1:
        for to in range(1, ntm):

            @pl.when(x < to)
            def _():
                state_copy(to, jnp.minimum(x, ntm - 2)).start()

        for src in range(ntm - 1):

            @pl.when(x > src)
            def _():
                state_copy(lax.rem(x + 1, ntm), src).wait_recv()

            @pl.when(x <= src)
            def _():
                st_recv[src] = jnp.zeros_like(st_send)

            length = (jnp.maximum(x - 1 - src, 0) * time_dev).astype(f32)
            pm = jnp.exp(-d * length)
            pr, pi = pm * jnp.cos(w * length), pm * jnp.sin(w * length)
            got_re, got_im = st_recv[src][:, 0:1], st_recv[src][:, 1:2]
            in_re = in_re + pr * got_re - pi * got_im
            in_im = in_im + pi * got_re + pr * got_im

    t_re, t_im = tabs[0], tabs[1]
    for blk in range(nb):
        y = loc[blk] + t_re * in_re - t_im * in_im
        cols = slice(blk * LANES, (blk + 1) * LANES)
        y_ref[:, cols] = y
        in_re, in_im = (
            zb_re * in_re - zb_im * in_im + end_re[blk],
            zb_im * in_re + zb_re * in_im + end_im[blk],
        )
        part = dot_split(ls, y)
        for j in range(owners):
            fs[j, :, cols] = part[j * fd : (j + 1) * fd]

    def motion_copy(k):
        j = lax.rem(me + k, owners)
        return pltpu.make_async_remote_copy(
            src_ref=fs.at[j], dst_ref=fr.at[me], send_sem=f_s.at[k], recv_sem=f_r.at[k],
            device_id={"taps": j // nc, "floors": lax.rem(j, nc)}, device_id_type=MESH,
        )

    def motion_start(k, carry):
        motion_copy(k).start()
        return carry

    def motion_recv(k, total):
        motion_copy(k).wait_recv()
        return total + fr[lax.rem(me + owners - k, owners)]

    def motion_sent(k, carry):
        motion_copy(k).wait_send()
        return carry

    lax.fori_loop(1, owners, motion_start, 0)
    load_scale = (floors / (taps * owners)) ** 0.5
    for h in range(nc):
        fl_ref[:, h * th : (h + 1) * th] = fb[h, md : md + fd, :] * load_scale

    for k in range(nch):
        pair_copy(k).wait_send()

    def line_sent(k, carry):
        @pl.when(z < nz - 1)
        def _():
            line_copy(k, True).wait_send()

        @pl.when(z > 0)
        def _():
            line_copy(k, False).wait_send()

        return carry

    lax.fori_loop(0, nch, line_sent, 0)
    ex.wait_send()
    for to in range(1, ntm):

        @pl.when(x < to)
        def _():
            state_copy(to, jnp.minimum(x, ntm - 2)).wait_send()

    fm_ref[...] = lax.fori_loop(1, owners, motion_recv, fs[me])
    lax.fori_loop(1, owners, motion_sent, 0)


def on_device(
    pressures, tap_area, tap_panel, tap_floor, panel_shape, floor_shape, mode_order, mode_decay, mode_freq
):
    nz, nc, ntm = lax.axis_size("taps"), lax.axis_size("floors"), lax.axis_size("tm")
    owners = nz * nc
    time_dev, taps = pressures.shape
    panels, modes = panel_shape.shape
    floors = floor_shape.shape[0]
    rows = panels + floors
    splits = 2
    th = time_dev // nc
    md, fd = modes // owners, floors // owners
    nch = th // LANES * splits
    xrows = md + -(-fd // 8) * 8
    chunk = pltpu.VMEM((nch, rows // splits, LANES), jnp.float32)
    vmem = pl.BlockSpec(memory_space=pltpu.VMEM)
    dma = pltpu.SemaphoreType.DMA
    f32 = jnp.float32
    out = pl.pallas_call(
        functools.partial(kernel, (nz, nc, ntm, splits)),
        out_shape=(
            jax.ShapeDtypeStruct((md, time_dev), f32),
            jax.ShapeDtypeStruct((fd, time_dev), f32),
            jax.ShapeDtypeStruct((fd, time_dev), f32),
        ),
        in_specs=[pl.BlockSpec(memory_space=pl.ANY)] + [vmem] * 8,
        out_specs=(vmem,) * 3,
        scratch_shapes=[
            pltpu.VMEM((time_dev, taps), jnp.bfloat16),
            pltpu.VMEM((rows, taps), jnp.bfloat16),
            chunk, chunk, chunk, chunk, chunk, chunk, chunk,
            pltpu.VMEM((xrows, th), f32),
            pltpu.VMEM((nc, xrows, th), f32),
            pltpu.VMEM((16, md, LANES), f32),
            pltpu.VMEM((time_dev // LANES, md, LANES), f32),
            pltpu.VMEM((md, LANES), f32),
            pltpu.VMEM((max(ntm - 1, 1), md, LANES), f32),
            pltpu.VMEM((owners, fd, time_dev), f32),
            pltpu.VMEM((owners, fd, time_dev), f32),
            dma((2 * (th // min(256, th)),)),
            dma((nch,)), dma((nch,)), dma((nch,)), dma((nch,)), dma((nch,)), dma((nch,)),
            dma, dma,
            dma((ntm,)), dma((ntm,)),
            dma((owners,)), dma((owners,)),
        ],
        compiler_params=pltpu.CompilerParams(
            collective_id=0, has_side_effects=True, vmem_limit_bytes=48 * 1024 * 1024
        ),
    )(
        pressures,
        tap_area.reshape(1, taps),
        tap_panel.reshape(1, taps),
        tap_floor.reshape(1, taps),
        panel_shape,
        floor_shape,
        mode_order.reshape(modes, 1),
        mode_decay.reshape(1, modes),
        mode_freq.reshape(1, modes),
    )
    return out


def solution(mesh):
    own = P(("taps", "floors"))
    out_spec = P(("taps", "floors"), ("dirs", "tm"))
    return jax.shard_map(
        on_device,
        mesh=mesh,
        in_specs=(P(("dirs", "tm"), ("taps", "floors")), own, own, own, P(), P(), P(), P(), P()),
        out_specs=(out_spec, out_spec, out_spec),
        check_vma=False,
    )
```

```python
import functools

import jax
import jax.numpy as jnp
from jax import lax
from jax.experimental import pallas as pl
from jax.experimental.pallas import tpu as pltpu
from jax.sharding import PartitionSpec as P

MESH = pl.DeviceIdType.MESH
LANES = 128
LAG = 2
NT = (((1,), (1,)), ((), ()))


def dot_nt(a, b):
    return lax.dot_general(a, b, NT, preferred_element_type=jnp.float32)


def dot_split(a, b):
    hi = b.astype(jnp.bfloat16)
    lo = (b - hi.astype(jnp.float32)).astype(jnp.bfloat16)
    return jnp.dot(a, hi, preferred_element_type=jnp.float32) + jnp.dot(
        a, lo, preferred_element_type=jnp.float32
    )


def kernel(
    cfg,
    p_hbm, area_h, panel_h, floor_h, shape_h, fshape_h, order_h, decay_h, freq_h,
    y_ref, fm_ref, fl_ref,
    area_ref, panel_ref, floor_ref, shape_ref, fshape_ref, order_ref, decay_ref, freq_ref, order_col,
    pv, w_ref, mine, send_p, recv_p, rin, lin, rout, lout, xs, fb, tabs, loc, loc_im, st_send, st_recv,
    fs, fr,
    in_sem, p_sem, pp_s, pp_r, r_s, r_r, l_s, l_r, x_s, x_r, t_s, t_r, f_s, f_r,
):
    nz, nc, ntm, splits = cfg
    owners = nz * nc
    z = lax.axis_index("taps")
    c = lax.axis_index("floors")
    x = lax.axis_index("tm")
    me = z * nc + c
    other = nc - 1 - c
    time_dev, taps = pv.shape
    panels, modes = shape_ref.shape
    floors = fshape_ref.shape[0]
    rows = panels + floors
    th = time_dev // nc
    tblocks = th // LANES
    crows = rows // splits
    nch = tblocks * splits
    md = modes // owners
    fd = floors // owners
    f32 = jnp.float32
    bf16 = jnp.bfloat16

    small = [
        pltpu.make_async_copy(src, dst, in_sem.at[i])
        for i, (src, dst) in enumerate(
            (
                (area_h, area_ref), (panel_h, panel_ref), (floor_h, floor_ref), (shape_h, shape_ref),
                (fshape_h, fshape_ref), (order_h, order_ref), (decay_h, decay_ref), (freq_h, freq_ref),
            )
        )
    ]
    for cp in small:
        cp.start()

    barrier = pltpu.get_barrier_semaphore()

    def greet(k, carry):
        j = lax.rem(me + k, owners)
        pl.semaphore_signal(
            barrier, inc=1, device_id={"taps": j // nc, "floors": lax.rem(j, nc)}, device_id_type=MESH
        )
        return carry

    lax.fori_loop(1, owners, greet, 0)
    for k in range(1, ntm):
        pl.semaphore_signal(
            barrier, inc=1, device_id={"tm": lax.rem(x + k, ntm)}, device_id_type=MESH
        )

    step_t = min(256, th)
    per_half = th // step_t
    loads = []
    for h in range(2):
        half = other if h == 0 else c
        for b in range(per_half):
            off = pl.multiple_of(half * th + b * step_t, step_t)
            cp = pltpu.make_async_copy(
                p_hbm.at[pl.ds(off, step_t)], pv.at[pl.ds(off, step_t)], p_sem.at[h * per_half + b]
            )
            cp.start()
            loads.append((cp, off))

    for cp in small[:3]:
        cp.wait()
    ids = lax.broadcasted_iota(jnp.int32, (panels, LANES), 0)
    fids = lax.broadcasted_iota(jnp.int32, (floors, LANES), 0)
    area = area_ref[...].astype(f32)
    for r in range(taps // LANES):
        cols = slice(r * LANES, (r + 1) * LANES)
        row = area[r : r + 1, :]
        w_ref[0:panels, cols] = jnp.where(panel_ref[:, cols] == ids, row, 0.0).astype(bf16)
        w_ref[panels:rows, cols] = jnp.where(floor_ref[:, cols] == fids, row, 0.0).astype(bf16)

    def sums(b, h, dst):
        cp, off = loads[h * per_half + b]
        cp.wait()
        q = dot_nt(w_ref[...], pv[pl.ds(off, step_t), :])
        for i in range(step_t // LANES):
            for s in range(splits):
                dst[(b * step_t // LANES + i) * splits + s] = q[
                    s * crows : (s + 1) * crows, i * LANES : (i + 1) * LANES
                ]

    def pair_copy(k):
        return pltpu.make_async_remote_copy(
            src_ref=send_p.at[k], dst_ref=recv_p.at[k], send_sem=pp_s.at[k], recv_sem=pp_r.at[k],
            device_id={"floors": other}, device_id_type=MESH,
        )

    per_step = step_t // LANES * splits

    @pl.when(z == 0)
    def _():
        rin[...] = jnp.zeros_like(rin)

    @pl.when(z == nz - 1)
    def _():
        lin[...] = jnp.zeros_like(lin)

    def line_copy(k, right):
        src, dst, ss, rs = (rout, rin, r_s, r_r) if right else (lout, lin, l_s, l_r)
        to = jnp.minimum(z + 1, nz - 1) if right else jnp.maximum(z - 1, 0)
        return pltpu.make_async_remote_copy(
            src_ref=src.at[k], dst_ref=dst.at[k], send_sem=ss.at[k], recv_sem=rs.at[k],
            device_id={"taps": to}, device_id_type=MESH,
        )

    def line_step(s, carry):
        for right in (True, False):
            hop = z if right else nz - 1 - z
            k = s - LAG * hop
            came, out = (rin, rout) if right else (lin, lout)

            @pl.when(jnp.logical_and(k >= 0, k < nch))
            def _():
                @pl.when(hop > 0)
                def _():
                    line_copy(k, right).wait_recv()

                @pl.when(hop < nz - 1)
                def _():
                    out[k] = mine[k] + came[k]
                    line_copy(k, right).start()

        return carry

    def merge(b):
        for k in range(b * per_step, (b + 1) * per_step):
            pair_copy(k).wait_recv()
            mine[k] = mine[k] + recv_p[k]

    for b in range(per_half):
        sums(b, 0, send_p)
        if b == 0:
            pl.semaphore_wait(barrier, owners - 1 + ntm - 1)
        for k in range(b * per_step, (b + 1) * per_step):
            pair_copy(k).start()
        sums(b, 1, mine)
        if b > 0:
            merge(b - 1)
        if b == 1:
            lax.fori_loop(0, min(LAG, per_step), line_step, 0)
    merge(per_half - 1)
    first = min(LAG, per_step) if per_half > 1 else 0
    early = min(LAG + 2, nch)
    lax.fori_loop(first, early, line_step, 0)

    for cp in small[3:]:
        cp.wait()
    order_col[...] = jnp.transpose(jnp.broadcast_to(order_ref[...].astype(f32), (LANES, modes)))
    mode_ids = lax.broadcasted_iota(jnp.int32, (md, modes), 1).astype(f32)

    def pick(owner):
        return order_col[pl.ds(pl.multiple_of(owner * md, md), md), 0:1] == mode_ids

    def shapes(hot):
        return dot_nt(hot.astype(f32).astype(bf16), shape_ref[...]).astype(bf16)

    hot_me = pick(me)
    hot_other = pick(z * nc + other)
    g_both = jnp.concatenate([shapes(hot_other), shapes(hot_me)], axis=0)
    d = jnp.sum(jnp.where(hot_me, decay_ref[...], 0.0), axis=1, keepdims=True)
    w = jnp.sum(jnp.where(hot_me, freq_ref[...], 0.0), axis=1, keepdims=True)
    ls = dot_nt(fshape_ref[...], hot_me.astype(f32).astype(bf16)).astype(bf16)
    e2 = 2.0 * d
    poly = jnp.full_like(e2, 1.0 / 40320.0)
    for coef in (1.0 / 5040, 1.0 / 720, 1.0 / 120, 1.0 / 24, 1.0 / 6, 0.5, 1.0):
        poly = coef - e2 * poly
    gain = jnp.sqrt(e2 * poly)
    lane = lax.broadcasted_iota(jnp.int32, (md, LANES), 1)
    ahead = (lane + 1).astype(f32)
    mag = jnp.exp(-d * ahead)
    t_re = mag * jnp.cos(w * ahead)
    t_im = mag * jnp.sin(w * ahead)
    tabs[0] = t_re
    tabs[1] = t_im
    hops = []
    step = 1
    while step < LANES:
        i = 2 + 2 * len(hops)
        tabs[i] = jnp.where(lane >= step, t_re[:, step - 1 : step], 0.0)
        tabs[i + 1] = jnp.where(lane >= step, t_im[:, step - 1 : step], 0.0)
        hops.append(step)
        step *= 2

    floor_row = lax.broadcasted_iota(jnp.int32, (floors, LANES), 0)

    def load_row(q, row):
        return jnp.sum(jnp.where(floor_row == row, q, 0.0), axis=0, keepdims=True)

    def exchange(tb):
        return pltpu.make_async_remote_copy(
            src_ref=xs.at[tb], dst_ref=fb.at[c * tblocks + tb],
            send_sem=x_s.at[tb], recv_sem=x_r.at[tb],
            device_id={"floors": other}, device_id_type=MESH,
        )

    def forces(tb):
        q = jnp.concatenate(
            [mine[k] + rin[k] + lin[k] for k in range(tb * splits, (tb + 1) * splits)], axis=0
        )
        both = dot_split(g_both, q[:panels])
        blk = c * tblocks + tb
        pad = [jnp.zeros((xs.shape[1] - md - fd, LANES), f32)] if xs.shape[1] > md + fd else []
        theirs = [load_row(q[panels:], (z * nc + other) * fd + r) for r in range(fd)]
        ours = [load_row(q[panels:], me * fd + r) for r in range(fd)]
        xs[tb] = jnp.concatenate([both[:md]] + theirs + pad, axis=0)
        exchange(tb).start()
        fb[blk] = jnp.concatenate([both[md:]] + ours + pad, axis=0)

    def at_rest(blk):
        re = gain * fb[blk, 0:md, :]
        im = None
        for i, step in enumerate(hops):
            a, b = tabs[2 + 2 * i], tabs[3 + 2 * i]
            rr = pltpu.roll(re, step, 1)
            if im is None:
                re, im = re + a * rr, b * rr
            else:
                ri = pltpu.roll(im, step, 1)
                re, im = re + a * rr - b * ri, im + a * ri + b * rr
        loc[blk] = re
        loc_im[blk] = im

    done = early
    for tb in range(tblocks):
        upto = (tb + 1) * splits + LAG * (nz - 1)
        lax.fori_loop(done, upto, line_step, 0)
        done = upto
        forces(tb)
        at_rest(c * tblocks + tb)
        if tb > 0:
            exchange(tb - 1).wait_recv()
            at_rest(other * tblocks + tb - 1)
    exchange(tblocks - 1).wait_recv()
    at_rest(other * tblocks + tblocks - 1)
    nb = time_dev // LANES
    end_re = [loc[blk][:, LANES - 1 :] for blk in range(nb)]
    end_im = [loc_im[blk][:, LANES - 1 :] for blk in range(nb)]

    zb_re, zb_im = t_re[:, LANES - 1 :], t_im[:, LANES - 1 :]
    s_re, s_im = end_re[0], end_im[0]
    for blk in range(1, nb):
        s_re, s_im = (
            zb_re * s_re - zb_im * s_im + end_re[blk],
            zb_im * s_re + zb_re * s_im + end_im[blk],
        )

    def state_copy(to, src):
        return pltpu.make_async_remote_copy(
            src_ref=st_send, dst_ref=st_recv.at[src], send_sem=t_s.at[to], recv_sem=t_r.at[src],
            device_id={"tm": to}, device_id_type=MESH,
        )

    st_send[...] = jnp.where(lane == 0, s_re, s_im)
    in_re = jnp.zeros((md, 1), f32)
    in_im = jnp.zeros((md, 1), f32)
    if ntm > 1:
        for to in range(1, ntm):

            @pl.when(x < to)
            def _():
                state_copy(to, jnp.minimum(x, ntm - 2)).start()

        for src in range(ntm - 1):

            @pl.when(x > src)
            def _():
                state_copy(lax.rem(x + 1, ntm), src).wait_recv()

            @pl.when(x <= src)
            def _():
                st_recv[src] = jnp.zeros_like(st_send)

            length = (jnp.maximum(x - 1 - src, 0) * time_dev).astype(f32)
            pm = jnp.exp(-d * length)
            pr, pi = pm * jnp.cos(w * length), pm * jnp.sin(w * length)
            got_re, got_im = st_recv[src][:, 0:1], st_recv[src][:, 1:2]
            in_re = in_re + pr * got_re - pi * got_im
            in_im = in_im + pi * got_re + pr * got_im

    t_re, t_im = tabs[0], tabs[1]
    for blk in range(nb):
        y = loc[blk] + t_re * in_re - t_im * in_im
        cols = slice(blk * LANES, (blk + 1) * LANES)
        y_ref[:, cols] = y
        in_re, in_im = (
            zb_re * in_re - zb_im * in_im + end_re[blk],
            zb_im * in_re + zb_re * in_im + end_im[blk],
        )
        part = dot_split(ls, y)
        for j in range(owners):
            fs[j, :, cols] = part[j * fd : (j + 1) * fd]

    def motion_copy(k):
        j = lax.rem(me + k, owners)
        return pltpu.make_async_remote_copy(
            src_ref=fs.at[j], dst_ref=fr.at[me], send_sem=f_s.at[k], recv_sem=f_r.at[k],
            device_id={"taps": j // nc, "floors": lax.rem(j, nc)}, device_id_type=MESH,
        )

    def motion_start(k, carry):
        motion_copy(k).start()
        return carry

    def motion_recv(k, total):
        motion_copy(k).wait_recv()
        return total + fr[lax.rem(me + owners - k, owners)]

    def motion_sent(k, carry):
        motion_copy(k).wait_send()
        return carry

    lax.fori_loop(1, owners, motion_start, 0)
    load_scale = (floors / (taps * owners)) ** 0.5
    for blk in range(nb):
        fl_ref[:, blk * LANES : (blk + 1) * LANES] = fb[blk, md : md + fd, :] * load_scale

    for k in range(nch):
        pair_copy(k).wait_send()

    def line_sent(k, carry):
        @pl.when(z < nz - 1)
        def _():
            line_copy(k, True).wait_send()

        @pl.when(z > 0)
        def _():
            line_copy(k, False).wait_send()

        return carry

    lax.fori_loop(0, nch, line_sent, 0)
    for tb in range(tblocks):
        exchange(tb).wait_send()
    for to in range(1, ntm):

        @pl.when(x < to)
        def _():
            state_copy(to, jnp.minimum(x, ntm - 2)).wait_send()

    fm_ref[...] = lax.fori_loop(1, owners, motion_recv, fs[me])
    lax.fori_loop(1, owners, motion_sent, 0)


def write_out(y, fm, fl, y_out, fm_out, fl_out, sem):
    copies = [
        pltpu.make_async_copy(src, dst, sem.at[i])
        for i, (src, dst) in enumerate(((y, y_out), (fm, fm_out), (fl, fl_out)))
    ]
    for cp in copies:
        cp.start()
    for cp in copies:
        cp.wait()


def on_device(
    pressures, tap_area, tap_panel, tap_floor, panel_shape, floor_shape, mode_order, mode_decay, mode_freq
):
    nz, nc, ntm = lax.axis_size("taps"), lax.axis_size("floors"), lax.axis_size("tm")
    owners = nz * nc
    time_dev, taps = pressures.shape
    panels, modes = panel_shape.shape
    floors = floor_shape.shape[0]
    rows = panels + floors
    splits = 2
    th = time_dev // nc
    md, fd = modes // owners, floors // owners
    nch = th // LANES * splits
    xrows = md + -(-fd // 8) * 8
    chunk = pltpu.VMEM((nch, rows // splits, LANES), jnp.float32)
    vmem = pl.BlockSpec(memory_space=pltpu.VMEM)
    dma = pltpu.SemaphoreType.DMA
    f32 = jnp.float32
    out = pl.pallas_call(
        functools.partial(kernel, (nz, nc, ntm, splits)),
        out_shape=(
            jax.ShapeDtypeStruct((md, time_dev), f32),
            jax.ShapeDtypeStruct((fd, time_dev), f32),
            jax.ShapeDtypeStruct((fd, time_dev), f32),
        ),
        in_specs=[pl.BlockSpec(memory_space=pltpu.HBM)] * 9,
        out_specs=(vmem,) * 3,
        scratch_shapes=[
            pltpu.VMEM((taps // LANES, LANES), jnp.bfloat16),
            pltpu.VMEM((1, taps), jnp.int32),
            pltpu.VMEM((1, taps), jnp.int32),
            pltpu.VMEM(panel_shape.shape, jnp.bfloat16),
            pltpu.VMEM(floor_shape.shape, jnp.bfloat16),
            pltpu.VMEM((1, modes), jnp.int32),
            pltpu.VMEM((1, modes), f32),
            pltpu.VMEM((1, modes), f32),
            pltpu.VMEM((modes, LANES), f32),
            pltpu.VMEM((time_dev, taps), jnp.bfloat16),
            pltpu.VMEM((rows, taps), jnp.bfloat16),
            chunk, chunk, chunk, chunk, chunk, chunk, chunk,
            pltpu.VMEM((th // LANES, xrows, LANES), f32),
            pltpu.VMEM((time_dev // LANES, xrows, LANES), f32),
            pltpu.VMEM((16, md, LANES), f32),
            pltpu.VMEM((time_dev // LANES, md, LANES), f32),
            pltpu.VMEM((time_dev // LANES, md, LANES), f32),
            pltpu.VMEM((md, LANES), f32),
            pltpu.VMEM((max(ntm - 1, 1), md, LANES), f32),
            pltpu.VMEM((owners, fd, time_dev), f32),
            pltpu.VMEM((owners, fd, time_dev), f32),
            dma((8,)),
            dma((2 * (th // min(256, th)),)),
            dma((nch,)), dma((nch,)), dma((nch,)), dma((nch,)), dma((nch,)), dma((nch,)),
            dma((th // LANES,)), dma((th // LANES,)),
            dma((ntm,)), dma((ntm,)),
            dma((owners,)), dma((owners,)),
        ],
        compiler_params=pltpu.CompilerParams(
            collective_id=0, has_side_effects=True, vmem_limit_bytes=67043328
        ),
    )(
        pressures,
        tap_area.reshape(taps // LANES, LANES),
        tap_panel.reshape(1, taps),
        tap_floor.reshape(1, taps),
        panel_shape,
        floor_shape,
        mode_order.reshape(1, modes),
        mode_decay.reshape(1, modes),
        mode_freq.reshape(1, modes),
    )
    return pl.pallas_call(
        write_out,
        out_shape=tuple(jax.ShapeDtypeStruct(o.shape, o.dtype) for o in out),
        in_specs=[vmem] * 3,
        out_specs=(pl.BlockSpec(memory_space=pltpu.HBM),) * 3,
        scratch_shapes=[dma((3,))],
        compiler_params=pltpu.CompilerParams(vmem_limit_bytes=67043328),
    )(*out)


def solution(mesh):
    own = P(("taps", "floors"))
    out_spec = P(("taps", "floors"), ("dirs", "tm"))
    return jax.shard_map(
        on_device,
        mesh=mesh,
        in_specs=(P(("dirs", "tm"), ("taps", "floors")), own, own, own, P(), P(), P(), P(), P()),
        out_specs=(out_spec, out_spec, out_spec),
        check_vma=False,
    )
```

```python
import functools

import jax
import jax.numpy as jnp
from jax import lax
from jax.experimental import pallas as pl
from jax.experimental.pallas import tpu as pltpu
from jax.sharding import PartitionSpec as P

MESH = pl.DeviceIdType.MESH
LANES = 128
LAG = 2
NT = (((1,), (1,)), ((), ()))


def dot_nt(a, b):
    return lax.dot_general(a, b, NT, preferred_element_type=jnp.float32)


def dot_split(a, b):
    hi = b.astype(jnp.bfloat16)
    lo = (b - hi.astype(jnp.float32)).astype(jnp.bfloat16)
    return jnp.dot(a, hi, preferred_element_type=jnp.float32) + jnp.dot(
        a, lo, preferred_element_type=jnp.float32
    )


def kernel(
    cfg,
    p_hbm, area_h, panel_h, floor_h, shape_h, fshape_h, order_h, decay_h, freq_h,
    y_ref, fm_ref, fl_ref,
    area_ref, panel_ref, floor_ref, shape_ref, fshape_ref, order_ref, decay_ref, freq_ref, order_col,
    pv, w_ref, mine, send_p, recv_p, rin, lin, rout, lout, xs, fb, tabs, loc, loc_im, st_send, st_recv,
    fs, fr,
    in_sem, p_sem, pp_s, pp_r, r_s, r_r, l_s, l_r, x_s, x_r, t_s, t_r, f_s, f_r,
):
    nz, nc, ntm, splits = cfg
    owners = nz * nc
    z = lax.axis_index("taps")
    c = lax.axis_index("floors")
    x = lax.axis_index("tm")
    me = z * nc + c
    other = nc - 1 - c
    time_dev, taps = pv.shape
    panels, modes = shape_ref.shape
    floors = fshape_ref.shape[0]
    rows = panels + floors
    th = time_dev // nc
    tblocks = th // LANES
    crows = rows // splits
    nch = tblocks * splits
    md = modes // owners
    fd = floors // owners
    f32 = jnp.float32
    bf16 = jnp.bfloat16

    small = [
        pltpu.make_async_copy(src, dst, in_sem.at[i])
        for i, (src, dst) in enumerate(
            (
                (area_h, area_ref), (panel_h, panel_ref), (floor_h, floor_ref), (shape_h, shape_ref),
                (fshape_h, fshape_ref), (order_h, order_ref), (decay_h, decay_ref), (freq_h, freq_ref),
            )
        )
    ]
    for cp in small:
        cp.start()

    barrier = pltpu.get_barrier_semaphore()

    def greet(k, carry):
        j = lax.rem(me + k, owners)
        pl.semaphore_signal(
            barrier, inc=1, device_id={"taps": j // nc, "floors": lax.rem(j, nc)}, device_id_type=MESH
        )
        return carry

    lax.fori_loop(1, owners, greet, 0)
    for k in range(1, ntm):
        pl.semaphore_signal(
            barrier, inc=1, device_id={"tm": lax.rem(x + k, ntm)}, device_id_type=MESH
        )

    step_t = min(256, th)
    per_half = th // step_t
    loads = []
    for h in range(2):
        half = other if h == 0 else c
        for b in range(per_half):
            off = pl.multiple_of(half * th + b * step_t, step_t)
            cp = pltpu.make_async_copy(
                p_hbm.at[pl.ds(off, step_t)], pv.at[pl.ds(off, step_t)], p_sem.at[h * per_half + b]
            )
            cp.start()
            loads.append((cp, off))

    for cp in small[:3]:
        cp.wait()
    ids = lax.broadcasted_iota(jnp.int32, (panels, LANES), 0)
    fids = lax.broadcasted_iota(jnp.int32, (floors, LANES), 0)
    area = area_ref[...].astype(f32)
    for r in range(taps // LANES):
        cols = slice(r * LANES, (r + 1) * LANES)
        row = area[r : r + 1, :]
        w_ref[0:panels, cols] = jnp.where(panel_ref[:, cols] == ids, row, 0.0).astype(bf16)
        w_ref[panels:rows, cols] = jnp.where(floor_ref[:, cols] == fids, row, 0.0).astype(bf16)

    def sums(b, h, dst):
        cp, off = loads[h * per_half + b]
        cp.wait()
        q = dot_nt(w_ref[...], pv[pl.ds(off, step_t), :])
        for i in range(step_t // LANES):
            for s in range(splits):
                dst[(b * step_t // LANES + i) * splits + s] = q[
                    s * crows : (s + 1) * crows, i * LANES : (i + 1) * LANES
                ]

    def pair_copy(k):
        return pltpu.make_async_remote_copy(
            src_ref=send_p.at[k], dst_ref=recv_p.at[k], send_sem=pp_s.at[k], recv_sem=pp_r.at[k],
            device_id={"floors": other}, device_id_type=MESH,
        )

    per_step = step_t // LANES * splits

    @pl.when(z == 0)
    def _():
        rin[...] = jnp.zeros_like(rin)

    @pl.when(z == nz - 1)
    def _():
        lin[...] = jnp.zeros_like(lin)

    def line_copy(k, right):
        src, dst, ss, rs = (rout, rin, r_s, r_r) if right else (lout, lin, l_s, l_r)
        to = jnp.minimum(z + 1, nz - 1) if right else jnp.maximum(z - 1, 0)
        return pltpu.make_async_remote_copy(
            src_ref=src.at[k], dst_ref=dst.at[k], send_sem=ss.at[k], recv_sem=rs.at[k],
            device_id={"taps": to}, device_id_type=MESH,
        )

    def line_step(s, carry):
        for right in (True, False):
            hop = z if right else nz - 1 - z
            k = s - LAG * hop
            came, out = (rin, rout) if right else (lin, lout)

            @pl.when(jnp.logical_and(k >= 0, k < nch))
            def _():
                @pl.when(hop > 0)
                def _():
                    line_copy(k, right).wait_recv()

                @pl.when(hop < nz - 1)
                def _():
                    out[k] = mine[k] + came[k]
                    line_copy(k, right).start()

        return carry

    def merge(b):
        for k in range(b * per_step, (b + 1) * per_step):
            pair_copy(k).wait_recv()
            mine[k] = mine[k] + recv_p[k]

    for b in range(per_half):
        sums(b, 0, send_p)
        if b == 0:
            pl.semaphore_wait(barrier, owners - 1 + ntm - 1)
        for k in range(b * per_step, (b + 1) * per_step):
            pair_copy(k).start()
        if b > 0:
            merge(b - 1)
        if b == 1:
            lax.fori_loop(0, min(LAG, per_step), line_step, 0)
        sums(b, 1, mine)
    merge(per_half - 1)
    first = min(LAG, per_step) if per_half > 1 else 0
    early = min(LAG, nch)
    lax.fori_loop(first, early, line_step, 0)

    for cp in small[3:]:
        cp.wait()
    order_col[...] = jnp.transpose(jnp.broadcast_to(order_ref[...].astype(f32), (LANES, modes)))
    mode_ids = lax.broadcasted_iota(jnp.int32, (md, modes), 1).astype(f32)

    def pick(owner):
        return order_col[pl.ds(pl.multiple_of(owner * md, md), md), 0:1] == mode_ids

    def shapes(hot):
        return dot_nt(hot.astype(f32).astype(bf16), shape_ref[...]).astype(bf16)

    hot_me = pick(me)
    hot_other = pick(z * nc + other)
    g_both = jnp.concatenate([shapes(hot_other), shapes(hot_me)], axis=0)
    d = jnp.sum(jnp.where(hot_me, decay_ref[...], 0.0), axis=1, keepdims=True)
    w = jnp.sum(jnp.where(hot_me, freq_ref[...], 0.0), axis=1, keepdims=True)
    ls = dot_nt(fshape_ref[...], hot_me.astype(f32).astype(bf16)).astype(bf16)
    e2 = 2.0 * d
    poly = jnp.full_like(e2, 1.0 / 40320.0)
    for coef in (1.0 / 5040, 1.0 / 720, 1.0 / 120, 1.0 / 24, 1.0 / 6, 0.5, 1.0):
        poly = coef - e2 * poly
    gain = jnp.sqrt(e2 * poly)
    lane = lax.broadcasted_iota(jnp.int32, (md, LANES), 1)
    ahead = (lane + 1).astype(f32)
    mag = jnp.exp(-d * ahead)
    t_re = mag * jnp.cos(w * ahead)
    t_im = mag * jnp.sin(w * ahead)
    tabs[0] = t_re
    tabs[1] = t_im
    hops = []
    step = 1
    while step < LANES:
        i = 2 + 2 * len(hops)
        tabs[i] = jnp.where(lane >= step, t_re[:, step - 1 : step], 0.0)
        tabs[i + 1] = jnp.where(lane >= step, t_im[:, step - 1 : step], 0.0)
        hops.append(step)
        step *= 2

    floor_row = lax.broadcasted_iota(jnp.int32, (floors, LANES), 0)

    def load_row(q, row):
        return jnp.sum(jnp.where(floor_row == row, q, 0.0), axis=0, keepdims=True)

    def exchange(tb):
        return pltpu.make_async_remote_copy(
            src_ref=xs.at[tb], dst_ref=fb.at[c * tblocks + tb],
            send_sem=x_s.at[tb], recv_sem=x_r.at[tb],
            device_id={"floors": other}, device_id_type=MESH,
        )

    def forces(tb):
        q = jnp.concatenate(
            [mine[k] + rin[k] + lin[k] for k in range(tb * splits, (tb + 1) * splits)], axis=0
        )
        both = dot_split(g_both, q[:panels])
        blk = c * tblocks + tb
        pad = [jnp.zeros((xs.shape[1] - md - fd, LANES), f32)] if xs.shape[1] > md + fd else []
        theirs = [load_row(q[panels:], (z * nc + other) * fd + r) for r in range(fd)]
        ours = [load_row(q[panels:], me * fd + r) for r in range(fd)]
        xs[tb] = jnp.concatenate([both[:md]] + theirs + pad, axis=0)
        exchange(tb).start()
        fb[blk] = jnp.concatenate([both[md:]] + ours + pad, axis=0)

    def at_rest(blk):
        re = gain * fb[blk, 0:md, :]
        im = None
        for i, step in enumerate(hops):
            a, b = tabs[2 + 2 * i], tabs[3 + 2 * i]
            rr = pltpu.roll(re, step, 1)
            if im is None:
                re, im = re + a * rr, b * rr
            else:
                ri = pltpu.roll(im, step, 1)
                re, im = re + a * rr - b * ri, im + a * ri + b * rr
        loc[blk] = re
        loc_im[blk] = im

    done = early
    for tb in range(tblocks):
        upto = (tb + 1) * splits + LAG * (nz - 1)
        lax.fori_loop(done, upto, line_step, 0)
        done = upto
        forces(tb)
        at_rest(c * tblocks + tb)
        if tb > 0:
            exchange(tb - 1).wait_recv()
            at_rest(other * tblocks + tb - 1)
    exchange(tblocks - 1).wait_recv()
    at_rest(other * tblocks + tblocks - 1)
    nb = time_dev // LANES
    end_re = [loc[blk][:, LANES - 1 :] for blk in range(nb)]
    end_im = [loc_im[blk][:, LANES - 1 :] for blk in range(nb)]

    zb_re, zb_im = t_re[:, LANES - 1 :], t_im[:, LANES - 1 :]
    s_re, s_im = end_re[0], end_im[0]
    for blk in range(1, nb):
        s_re, s_im = (
            zb_re * s_re - zb_im * s_im + end_re[blk],
            zb_im * s_re + zb_re * s_im + end_im[blk],
        )

    def state_copy(to, src):
        return pltpu.make_async_remote_copy(
            src_ref=st_send, dst_ref=st_recv.at[src], send_sem=t_s.at[to], recv_sem=t_r.at[src],
            device_id={"tm": to}, device_id_type=MESH,
        )

    st_send[...] = jnp.where(lane == 0, s_re, s_im)
    in_re = jnp.zeros((md, 1), f32)
    in_im = jnp.zeros((md, 1), f32)
    if ntm > 1:
        for to in range(1, ntm):

            @pl.when(x < to)
            def _():
                state_copy(to, jnp.minimum(x, ntm - 2)).start()

        for src in range(ntm - 1):

            @pl.when(x > src)
            def _():
                state_copy(lax.rem(x + 1, ntm), src).wait_recv()

            @pl.when(x <= src)
            def _():
                st_recv[src] = jnp.zeros_like(st_send)

            got_re, got_im = st_recv[src][:, 0:1], st_recv[src][:, 1:2]
            if ntm == 2:
                in_re, in_im = got_re, got_im
                continue
            length = (jnp.maximum(x - 1 - src, 0) * time_dev).astype(f32)
            pm = jnp.exp(-d * length)
            pr, pi = pm * jnp.cos(w * length), pm * jnp.sin(w * length)
            in_re = in_re + pr * got_re - pi * got_im
            in_im = in_im + pi * got_re + pr * got_im

    t_re, t_im = tabs[0], tabs[1]
    for blk in range(nb):
        y = loc[blk] + t_re * in_re - t_im * in_im
        cols = slice(blk * LANES, (blk + 1) * LANES)
        y_ref[:, cols] = y
        in_re, in_im = (
            zb_re * in_re - zb_im * in_im + end_re[blk],
            zb_im * in_re + zb_re * in_im + end_im[blk],
        )
    part = dot_split(ls, y_ref[...])
    for j in range(owners):
        fs[j] = part[j * fd : (j + 1) * fd]

    def motion_copy(k):
        j = lax.rem(me + k, owners)
        return pltpu.make_async_remote_copy(
            src_ref=fs.at[j], dst_ref=fr.at[me], send_sem=f_s.at[k], recv_sem=f_r.at[k],
            device_id={"taps": j // nc, "floors": lax.rem(j, nc)}, device_id_type=MESH,
        )

    def motion_start(k, carry):
        motion_copy(k).start()
        return carry

    def motion_recv(k, total):
        motion_copy(k).wait_recv()
        return total + fr[lax.rem(me + owners - k, owners)]

    def motion_sent(k, carry):
        motion_copy(k).wait_send()
        return carry

    lax.fori_loop(1, owners, motion_start, 0)
    load_scale = (floors / (taps * owners)) ** 0.5
    for blk in range(nb):
        fl_ref[:, blk * LANES : (blk + 1) * LANES] = fb[blk, md : md + fd, :] * load_scale

    for k in range(nch):
        pair_copy(k).wait_send()

    def line_sent(k, carry):
        @pl.when(z < nz - 1)
        def _():
            line_copy(k, True).wait_send()

        @pl.when(z > 0)
        def _():
            line_copy(k, False).wait_send()

        return carry

    lax.fori_loop(0, nch, line_sent, 0)
    for tb in range(tblocks):
        exchange(tb).wait_send()
    for to in range(1, ntm):

        @pl.when(x < to)
        def _():
            state_copy(to, jnp.minimum(x, ntm - 2)).wait_send()

    fm_ref[...] = lax.fori_loop(1, owners, motion_recv, fs[me])
    lax.fori_loop(1, owners, motion_sent, 0)


def write_out(y, fm, fl, y_out, fm_out, fl_out, sem):
    copies = [
        pltpu.make_async_copy(src, dst, sem.at[i])
        for i, (src, dst) in enumerate(((y, y_out), (fm, fm_out), (fl, fl_out)))
    ]
    for cp in copies:
        cp.start()
    for cp in copies:
        cp.wait()


def on_device(
    pressures, tap_area, tap_panel, tap_floor, panel_shape, floor_shape, mode_order, mode_decay, mode_freq
):
    nz, nc, ntm = lax.axis_size("taps"), lax.axis_size("floors"), lax.axis_size("tm")
    owners = nz * nc
    time_dev, taps = pressures.shape
    panels, modes = panel_shape.shape
    floors = floor_shape.shape[0]
    rows = panels + floors
    splits = 2
    th = time_dev // nc
    md, fd = modes // owners, floors // owners
    nch = th // LANES * splits
    xrows = md + -(-fd // 8) * 8
    chunk = pltpu.VMEM((nch, rows // splits, LANES), jnp.float32)
    vmem = pl.BlockSpec(memory_space=pltpu.VMEM)
    dma = pltpu.SemaphoreType.DMA
    f32 = jnp.float32
    out = pl.pallas_call(
        functools.partial(kernel, (nz, nc, ntm, splits)),
        out_shape=(
            jax.ShapeDtypeStruct((md, time_dev), f32),
            jax.ShapeDtypeStruct((fd, time_dev), f32),
            jax.ShapeDtypeStruct((fd, time_dev), f32),
        ),
        in_specs=[pl.BlockSpec(memory_space=pltpu.HBM)] * 9,
        out_specs=(vmem,) * 3,
        scratch_shapes=[
            pltpu.VMEM((taps // LANES, LANES), jnp.bfloat16),
            pltpu.VMEM((1, taps), jnp.int32),
            pltpu.VMEM((1, taps), jnp.int32),
            pltpu.VMEM(panel_shape.shape, jnp.bfloat16),
            pltpu.VMEM(floor_shape.shape, jnp.bfloat16),
            pltpu.VMEM((1, modes), jnp.int32),
            pltpu.VMEM((1, modes), f32),
            pltpu.VMEM((1, modes), f32),
            pltpu.VMEM((modes, LANES), f32),
            pltpu.VMEM((time_dev, taps), jnp.bfloat16),
            pltpu.VMEM((rows, taps), jnp.bfloat16),
            chunk, chunk, chunk, chunk, chunk, chunk, chunk,
            pltpu.VMEM((th // LANES, xrows, LANES), f32),
            pltpu.VMEM((time_dev // LANES, xrows, LANES), f32),
            pltpu.VMEM((16, md, LANES), f32),
            pltpu.VMEM((time_dev // LANES, md, LANES), f32),
            pltpu.VMEM((time_dev // LANES, md, LANES), f32),
            pltpu.VMEM((md, LANES), f32),
            pltpu.VMEM((max(ntm - 1, 1), md, LANES), f32),
            pltpu.VMEM((owners, fd, time_dev), f32),
            pltpu.VMEM((owners, fd, time_dev), f32),
            dma((8,)),
            dma((2 * (th // min(256, th)),)),
            dma((nch,)), dma((nch,)), dma((nch,)), dma((nch,)), dma((nch,)), dma((nch,)),
            dma((th // LANES,)), dma((th // LANES,)),
            dma((ntm,)), dma((ntm,)),
            dma((owners,)), dma((owners,)),
        ],
        compiler_params=pltpu.CompilerParams(
            collective_id=0, has_side_effects=True, vmem_limit_bytes=67043328
        ),
    )(
        pressures,
        tap_area.reshape(taps // LANES, LANES),
        tap_panel.reshape(1, taps),
        tap_floor.reshape(1, taps),
        panel_shape,
        floor_shape,
        mode_order.reshape(1, modes),
        mode_decay.reshape(1, modes),
        mode_freq.reshape(1, modes),
    )
    return pl.pallas_call(
        write_out,
        out_shape=tuple(jax.ShapeDtypeStruct(o.shape, o.dtype) for o in out),
        in_specs=[vmem] * 3,
        out_specs=(pl.BlockSpec(memory_space=pltpu.HBM),) * 3,
        scratch_shapes=[dma((3,))],
        compiler_params=pltpu.CompilerParams(vmem_limit_bytes=67043328),
    )(*out)


def solution(mesh):
    own = P(("taps", "floors"))
    out_spec = P(("taps", "floors"), ("dirs", "tm"))
    return jax.shard_map(
        on_device,
        mesh=mesh,
        in_specs=(P(("dirs", "tm"), ("taps", "floors")), own, own, own, P(), P(), P(), P(), P()),
        out_specs=(out_spec, out_spec, out_spec),
        check_vma=False,
    )
```

```python
import functools

import jax
import jax.numpy as jnp
from jax import lax
from jax.experimental import pallas as pl
from jax.experimental.pallas import tpu as pltpu
from jax.sharding import PartitionSpec as P

MESH = pl.DeviceIdType.MESH
LANES = 128
LAG = 2
NT = (((1,), (1,)), ((), ()))


def dot_nt(a, b):
    return lax.dot_general(a, b, NT, preferred_element_type=jnp.float32)


def dot_split(a, b):
    hi = b.astype(jnp.bfloat16)
    lo = (b - hi.astype(jnp.float32)).astype(jnp.bfloat16)
    return jnp.dot(a, hi, preferred_element_type=jnp.float32) + jnp.dot(
        a, lo, preferred_element_type=jnp.float32
    )


def kernel(
    cfg,
    p_hbm, area_h, panel_h, floor_h, shape_h, fshape_h, order_h, decay_h, freq_h,
    y_ref, fm_ref, fl_ref,
    area_ref, panel_ref, floor_ref, shape_ref, fshape_ref, order_ref, decay_ref, freq_ref, order_col,
    pv, w_ref, mine, send_p, recv_p, rin, lin, rout, lout, xs, fb, tabs, loc, loc_im, st_send, st_recv,
    fs, fr,
    in_sem, p_sem, pp_s, pp_r, r_s, r_r, l_s, l_r, x_s, x_r, t_s, t_r, f_s, f_r,
):
    nz, nc, ntm, splits = cfg
    owners = nz * nc
    z = lax.axis_index("taps")
    c = lax.axis_index("floors")
    x = lax.axis_index("tm")
    me = z * nc + c
    other = nc - 1 - c
    time_dev, taps = pv.shape
    panels, modes = shape_ref.shape
    floors = fshape_ref.shape[0]
    rows = panels + floors
    th = time_dev // nc
    tblocks = th // LANES
    crows = rows // splits
    nch = tblocks * splits
    md = modes // owners
    fd = floors // owners
    f32 = jnp.float32
    bf16 = jnp.bfloat16

    small = [
        pltpu.make_async_copy(src, dst, in_sem.at[i])
        for i, (src, dst) in enumerate(
            (
                (area_h, area_ref), (panel_h, panel_ref), (floor_h, floor_ref), (shape_h, shape_ref),
                (fshape_h, fshape_ref), (order_h, order_ref), (decay_h, decay_ref), (freq_h, freq_ref),
            )
        )
    ]
    for cp in small:
        cp.start()

    barrier = pltpu.get_barrier_semaphore()

    def greet(k, carry):
        j = lax.rem(me + k, owners)
        pl.semaphore_signal(
            barrier, inc=1, device_id={"taps": j // nc, "floors": lax.rem(j, nc)}, device_id_type=MESH
        )
        return carry

    lax.fori_loop(1, owners, greet, 0)
    for k in range(1, ntm):
        pl.semaphore_signal(
            barrier, inc=1, device_id={"tm": lax.rem(x + k, ntm)}, device_id_type=MESH
        )

    step_t = min(256, th)
    per_half = th // step_t
    loads = []
    for h in range(2):
        half = other if h == 0 else c
        for b in range(per_half):
            off = pl.multiple_of(half * th + b * step_t, step_t)
            cp = pltpu.make_async_copy(
                p_hbm.at[pl.ds(off, step_t)], pv.at[pl.ds(off, step_t)], p_sem.at[h * per_half + b]
            )
            cp.start()
            loads.append((cp, off))

    for cp in small[:3]:
        cp.wait()
    ids = lax.broadcasted_iota(jnp.int32, (panels, LANES), 0)
    fids = lax.broadcasted_iota(jnp.int32, (floors, LANES), 0)
    area = area_ref[...].astype(f32)
    for r in range(taps // LANES):
        cols = slice(r * LANES, (r + 1) * LANES)
        row = area[r : r + 1, :]
        w_ref[0:panels, cols] = jnp.where(panel_ref[:, cols] == ids, row, 0.0).astype(bf16)
        w_ref[panels:rows, cols] = jnp.where(floor_ref[:, cols] == fids, row, 0.0).astype(bf16)

    def sums(b, h, dst):
        cp, off = loads[h * per_half + b]
        cp.wait()
        q = dot_nt(w_ref[...], pv[pl.ds(off, step_t), :])
        for i in range(step_t // LANES):
            for s in range(splits):
                dst[(b * step_t // LANES + i) * splits + s] = q[
                    s * crows : (s + 1) * crows, i * LANES : (i + 1) * LANES
                ]

    def pair_copy(k):
        return pltpu.make_async_remote_copy(
            src_ref=send_p.at[k], dst_ref=recv_p.at[k], send_sem=pp_s.at[k], recv_sem=pp_r.at[k],
            device_id={"floors": other}, device_id_type=MESH,
        )

    per_step = step_t // LANES * splits

    @pl.when(z == 0)
    def _():
        rin[...] = jnp.zeros_like(rin)

    @pl.when(z == nz - 1)
    def _():
        lin[...] = jnp.zeros_like(lin)

    def line_copy(k, right):
        src, dst, ss, rs = (rout, rin, r_s, r_r) if right else (lout, lin, l_s, l_r)
        to = jnp.minimum(z + 1, nz - 1) if right else jnp.maximum(z - 1, 0)
        return pltpu.make_async_remote_copy(
            src_ref=src.at[k], dst_ref=dst.at[k], send_sem=ss.at[k], recv_sem=rs.at[k],
            device_id={"taps": to}, device_id_type=MESH,
        )

    def line_step(s, carry):
        for right in (True, False):
            hop = z if right else nz - 1 - z
            k = s - LAG * hop
            came, out = (rin, rout) if right else (lin, lout)

            @pl.when(jnp.logical_and(k >= 0, k < nch))
            def _():
                @pl.when(hop > 0)
                def _():
                    line_copy(k, right).wait_recv()

                @pl.when(hop < nz - 1)
                def _():
                    out[k] = mine[k] + came[k]
                    line_copy(k, right).start()

        return carry

    def merge(b):
        for k in range(b * per_step, (b + 1) * per_step):
            pair_copy(k).wait_recv()
            mine[k] = mine[k] + recv_p[k]

    for b in range(per_half):
        sums(b, 0, send_p)
        if b == 0:
            pl.semaphore_wait(barrier, owners - 1 + ntm - 1)
        for k in range(b * per_step, (b + 1) * per_step):
            pair_copy(k).start()
        if b > 0:
            merge(b - 1)
        if b == 1:
            lax.fori_loop(0, min(LAG, per_step), line_step, 0)
        sums(b, 1, mine)
    merge(per_half - 1)
    first = min(LAG, per_step) if per_half > 1 else 0
    early = min(LAG, nch)
    lax.fori_loop(first, early, line_step, 0)

    for cp in small[3:]:
        cp.wait()
    order_col[...] = jnp.transpose(jnp.broadcast_to(order_ref[...].astype(f32), (LANES, modes)))
    mode_ids = lax.broadcasted_iota(jnp.int32, (md, modes), 1).astype(f32)

    def pick(owner):
        return order_col[pl.ds(pl.multiple_of(owner * md, md), md), 0:1] == mode_ids

    def shapes(hot):
        return dot_nt(hot.astype(f32).astype(bf16), shape_ref[...]).astype(bf16)

    hot_me = pick(me)
    hot_other = pick(z * nc + other)
    g_both = jnp.concatenate([shapes(hot_other), shapes(hot_me)], axis=0)
    d = jnp.sum(jnp.where(hot_me, decay_ref[...], 0.0), axis=1, keepdims=True)
    w = jnp.sum(jnp.where(hot_me, freq_ref[...], 0.0), axis=1, keepdims=True)
    ls = dot_nt(fshape_ref[...], hot_me.astype(f32).astype(bf16)).astype(bf16)
    e2 = 2.0 * d
    poly = jnp.full_like(e2, 1.0 / 40320.0)
    for coef in (1.0 / 5040, 1.0 / 720, 1.0 / 120, 1.0 / 24, 1.0 / 6, 0.5, 1.0):
        poly = coef - e2 * poly
    gain = jnp.sqrt(e2 * poly)
    lane = lax.broadcasted_iota(jnp.int32, (md, LANES), 1)
    ahead = (lane + 1).astype(f32)
    mag = jnp.exp(-d * ahead)
    t_re = mag * jnp.cos(w * ahead)
    t_im = mag * jnp.sin(w * ahead)
    tabs[0] = t_re
    tabs[1] = t_im
    hops = []
    step = 1
    while step < LANES:
        i = 2 + 2 * len(hops)
        tabs[i] = jnp.where(lane >= step, t_re[:, step - 1 : step], 0.0)
        tabs[i + 1] = jnp.where(lane >= step, t_im[:, step - 1 : step], 0.0)
        hops.append(step)
        step *= 2

    floor_row = lax.broadcasted_iota(jnp.int32, (floors, LANES), 0)

    def load_row(q, row):
        return jnp.sum(jnp.where(floor_row == row, q, 0.0), axis=0, keepdims=True)

    def exchange(tb):
        return pltpu.make_async_remote_copy(
            src_ref=xs.at[tb], dst_ref=fb.at[c * tblocks + tb],
            send_sem=x_s.at[tb], recv_sem=x_r.at[tb],
            device_id={"floors": other}, device_id_type=MESH,
        )

    def forces(tb):
        q = jnp.concatenate(
            [mine[k] + rin[k] + lin[k] for k in range(tb * splits, (tb + 1) * splits)], axis=0
        )
        both = dot_split(g_both, q[:panels])
        blk = c * tblocks + tb
        pad = [jnp.zeros((xs.shape[1] - md - fd, LANES), f32)] if xs.shape[1] > md + fd else []
        theirs = [load_row(q[panels:], (z * nc + other) * fd + r) for r in range(fd)]
        ours = [load_row(q[panels:], me * fd + r) for r in range(fd)]
        xs[tb] = jnp.concatenate([both[:md]] + theirs + pad, axis=0)
        exchange(tb).start()
        fb[blk] = jnp.concatenate([both[md:]] + ours + pad, axis=0)

    def at_rest(blk):
        re = gain * fb[blk, 0:md, :]
        im = None
        for i, step in enumerate(hops):
            a, b = tabs[2 + 2 * i], tabs[3 + 2 * i]
            rr = pltpu.roll(re, step, 1)
            if im is None:
                re, im = re + a * rr, b * rr
            else:
                ri = pltpu.roll(im, step, 1)
                re, im = re + a * rr - b * ri, im + a * ri + b * rr
        loc[blk] = re
        loc_im[blk] = im

    done = early
    for tb in range(tblocks):
        upto = max((tb + 1) * splits + LAG * (nz - 1), nch + LAG * (nz - 2))
        lax.fori_loop(done, upto, line_step, 0)
        done = upto
        forces(tb)
        at_rest(c * tblocks + tb)
        if tb > 0:
            exchange(tb - 1).wait_recv()
            at_rest(other * tblocks + tb - 1)
    exchange(tblocks - 1).wait_recv()
    at_rest(other * tblocks + tblocks - 1)
    nb = time_dev // LANES
    end_re = [loc[blk][:, LANES - 1 :] for blk in range(nb)]
    end_im = [loc_im[blk][:, LANES - 1 :] for blk in range(nb)]

    zb_re, zb_im = t_re[:, LANES - 1 :], t_im[:, LANES - 1 :]
    s_re, s_im = end_re[0], end_im[0]
    for blk in range(1, nb):
        s_re, s_im = (
            zb_re * s_re - zb_im * s_im + end_re[blk],
            zb_im * s_re + zb_re * s_im + end_im[blk],
        )

    def state_copy(to, src):
        return pltpu.make_async_remote_copy(
            src_ref=st_send, dst_ref=st_recv.at[src], send_sem=t_s.at[to], recv_sem=t_r.at[src],
            device_id={"tm": to}, device_id_type=MESH,
        )

    st_send[...] = jnp.where(lane == 0, s_re, s_im)
    in_re = jnp.zeros((md, 1), f32)
    in_im = jnp.zeros((md, 1), f32)
    if ntm > 1:
        for to in range(1, ntm):

            @pl.when(x < to)
            def _():
                state_copy(to, jnp.minimum(x, ntm - 2)).start()

        for src in range(ntm - 1):

            @pl.when(x > src)
            def _():
                state_copy(lax.rem(x + 1, ntm), src).wait_recv()

            @pl.when(x <= src)
            def _():
                st_recv[src] = jnp.zeros_like(st_send)

            got_re, got_im = st_recv[src][:, 0:1], st_recv[src][:, 1:2]
            if ntm == 2:
                in_re, in_im = got_re, got_im
                continue
            length = (jnp.maximum(x - 1 - src, 0) * time_dev).astype(f32)
            pm = jnp.exp(-d * length)
            pr, pi = pm * jnp.cos(w * length), pm * jnp.sin(w * length)
            in_re = in_re + pr * got_re - pi * got_im
            in_im = in_im + pi * got_re + pr * got_im

    t_re, t_im = tabs[0], tabs[1]
    for blk in range(nb):
        y = loc[blk] + t_re * in_re - t_im * in_im
        cols = slice(blk * LANES, (blk + 1) * LANES)
        y_ref[:, cols] = y
        in_re, in_im = (
            zb_re * in_re - zb_im * in_im + end_re[blk],
            zb_im * in_re + zb_re * in_im + end_im[blk],
        )
    part = dot_split(ls, y_ref[...])
    for j in range(owners):
        fs[j] = part[j * fd : (j + 1) * fd]

    def motion_copy(k):
        j = lax.rem(me + k, owners)
        return pltpu.make_async_remote_copy(
            src_ref=fs.at[j], dst_ref=fr.at[me], send_sem=f_s.at[k], recv_sem=f_r.at[k],
            device_id={"taps": j // nc, "floors": lax.rem(j, nc)}, device_id_type=MESH,
        )

    def motion_start(k, carry):
        motion_copy(k).start()
        return carry

    def motion_recv(k, total):
        motion_copy(k).wait_recv()
        return total + fr[lax.rem(me + owners - k, owners)]

    def motion_sent(k, carry):
        motion_copy(k).wait_send()
        return carry

    lax.fori_loop(1, owners, motion_start, 0)
    load_scale = (floors / (taps * owners)) ** 0.5
    for blk in range(nb):
        fl_ref[:, blk * LANES : (blk + 1) * LANES] = fb[blk, md : md + fd, :] * load_scale

    for k in range(nch):
        pair_copy(k).wait_send()

    def line_sent(k, carry):
        @pl.when(z < nz - 1)
        def _():
            line_copy(k, True).wait_send()

        @pl.when(z > 0)
        def _():
            line_copy(k, False).wait_send()

        return carry

    lax.fori_loop(0, nch, line_sent, 0)
    for tb in range(tblocks):
        exchange(tb).wait_send()
    for to in range(1, ntm):

        @pl.when(x < to)
        def _():
            state_copy(to, jnp.minimum(x, ntm - 2)).wait_send()

    fm_ref[...] = lax.fori_loop(1, owners, motion_recv, fs[me])
    lax.fori_loop(1, owners, motion_sent, 0)


def write_out(y, fm, fl, y_out, fm_out, fl_out, sem):
    copies = [
        pltpu.make_async_copy(src, dst, sem.at[i])
        for i, (src, dst) in enumerate(((y, y_out), (fm, fm_out), (fl, fl_out)))
    ]
    for cp in copies:
        cp.start()
    for cp in copies:
        cp.wait()


def on_device(
    pressures, tap_area, tap_panel, tap_floor, panel_shape, floor_shape, mode_order, mode_decay, mode_freq
):
    nz, nc, ntm = lax.axis_size("taps"), lax.axis_size("floors"), lax.axis_size("tm")
    owners = nz * nc
    time_dev, taps = pressures.shape
    panels, modes = panel_shape.shape
    floors = floor_shape.shape[0]
    rows = panels + floors
    splits = 2
    th = time_dev // nc
    md, fd = modes // owners, floors // owners
    nch = th // LANES * splits
    xrows = md + -(-fd // 8) * 8
    chunk = pltpu.VMEM((nch, rows // splits, LANES), jnp.float32)
    vmem = pl.BlockSpec(memory_space=pltpu.VMEM)
    dma = pltpu.SemaphoreType.DMA
    f32 = jnp.float32
    out = pl.pallas_call(
        functools.partial(kernel, (nz, nc, ntm, splits)),
        out_shape=(
            jax.ShapeDtypeStruct((md, time_dev), f32),
            jax.ShapeDtypeStruct((fd, time_dev), f32),
            jax.ShapeDtypeStruct((fd, time_dev), f32),
        ),
        in_specs=[pl.BlockSpec(memory_space=pltpu.HBM)] * 9,
        out_specs=(vmem,) * 3,
        scratch_shapes=[
            pltpu.VMEM((taps // LANES, LANES), jnp.bfloat16),
            pltpu.VMEM((1, taps), jnp.int32),
            pltpu.VMEM((1, taps), jnp.int32),
            pltpu.VMEM(panel_shape.shape, jnp.bfloat16),
            pltpu.VMEM(floor_shape.shape, jnp.bfloat16),
            pltpu.VMEM((1, modes), jnp.int32),
            pltpu.VMEM((1, modes), f32),
            pltpu.VMEM((1, modes), f32),
            pltpu.VMEM((modes, LANES), f32),
            pltpu.VMEM((time_dev, taps), jnp.bfloat16),
            pltpu.VMEM((rows, taps), jnp.bfloat16),
            chunk, chunk, chunk, chunk, chunk, chunk, chunk,
            pltpu.VMEM((th // LANES, xrows, LANES), f32),
            pltpu.VMEM((time_dev // LANES, xrows, LANES), f32),
            pltpu.VMEM((16, md, LANES), f32),
            pltpu.VMEM((time_dev // LANES, md, LANES), f32),
            pltpu.VMEM((time_dev // LANES, md, LANES), f32),
            pltpu.VMEM((md, LANES), f32),
            pltpu.VMEM((max(ntm - 1, 1), md, LANES), f32),
            pltpu.VMEM((owners, fd, time_dev), f32),
            pltpu.VMEM((owners, fd, time_dev), f32),
            dma((8,)),
            dma((2 * (th // min(256, th)),)),
            dma((nch,)), dma((nch,)), dma((nch,)), dma((nch,)), dma((nch,)), dma((nch,)),
            dma((th // LANES,)), dma((th // LANES,)),
            dma((ntm,)), dma((ntm,)),
            dma((owners,)), dma((owners,)),
        ],
        compiler_params=pltpu.CompilerParams(
            collective_id=0, has_side_effects=True, vmem_limit_bytes=67043328
        ),
    )(
        pressures,
        tap_area.reshape(taps // LANES, LANES),
        tap_panel.reshape(1, taps),
        tap_floor.reshape(1, taps),
        panel_shape,
        floor_shape,
        mode_order.reshape(1, modes),
        mode_decay.reshape(1, modes),
        mode_freq.reshape(1, modes),
    )
    return pl.pallas_call(
        write_out,
        out_shape=tuple(jax.ShapeDtypeStruct(o.shape, o.dtype) for o in out),
        in_specs=[vmem] * 3,
        out_specs=(pl.BlockSpec(memory_space=pltpu.HBM),) * 3,
        scratch_shapes=[dma((3,))],
        compiler_params=pltpu.CompilerParams(vmem_limit_bytes=67043328),
    )(*out)


def solution(mesh):
    own = P(("taps", "floors"))
    out_spec = P(("taps", "floors"), ("dirs", "tm"))
    return jax.shard_map(
        on_device,
        mesh=mesh,
        in_specs=(P(("dirs", "tm"), ("taps", "floors")), own, own, own, P(), P(), P(), P(), P()),
        out_specs=(out_spec, out_spec, out_spec),
        check_vma=False,
    )
```
